32 devices in a mesh: day: 2 (over x), stn: 16 (over z, y, core).
Axes of the slice: x: 2, y: 2, z: 4, core: 2. Of those that a mesh axis runs over, the one named last changes fastest.
Arguments:
- station_partials: bfloat16 [131072, 128], P(('day', 'stn')), parts along dimension 0, may hold values from -6 to 6
- arc_partials: bfloat16 [131072, 128], P(('day', 'stn')), parts along dimension 0, may hold values from -6 to 6
- misclosure: bfloat16 [131072], P(('day', 'stn')), parts along dimension 0, may hold values from -6 to 6
- arc_id: int32 [131072, 1], P(('day', 'stn')), parts along dimension 0, may hold values from 0 to 31; in each aligned block of 4096 rows (0 to 4095, 4096 to 8191, ...) at most 256 rows name the same one
- arc_slot: int32 [64], P('day'), parts along dimension 0, may hold values from 0 to 31, each once
- arc_prior: float32 [64], P('day'), parts along dimension 0, may hold values from 0.1 to 1
Outputs:
- station_normal: float32 [32, 128, 128], P(('day', 'stn')), parts along dimension 0
- elimination: float32 [32, 128, 128], P(('day', 'stn')), parts along dimension 0
- elimination_rhs: float32 [32, 128], P(('day', 'stn')), parts along dimension 0
- arc_whitened: float32 [64, 128], P(('day', 'stn')), parts along dimension 0
The draws below stay inside these ranges and needn't reach their ends.
There are 2 independent parts, one for each index of `day`. The reference program is written for one: setup_inputs(seed, part) draws one part's arguments, and reference() takes and returns one part's arrays. A program takes and returns all parts, laid end to end along the dimension named above; each array names one. Nothing has to cross between parts.
Inputs may be any that keep to these rules, and one draw needn't show every extreme that they name: `arc_id`: among the rows of one station no arc is named more than 256 times, and in every day some station names some arc exactly 256 times; every arc is seen by some station. `arc_slot`: each slot is given to exactly one arc.
All inputs are finite; a program needn't handle non-finite values.
Results may differ from the reference program's by a relative error of at most 0.0003.
Values may be sent and summed in bfloat16 or wider, within the bound.
No kernel may reach another device: no remote copies, remote signals or barrier semaphores. Data moves between devices by JAX's collectives and lax.ppermute only.
A program may use at most 128 MiB of HBM per device.

```python
import math
import jax
import jax.numpy as jnp
import numpy as np
from jax import lax

P_SIZE = 128
OBS_DEV = 4096
ARCS = 32
CAP = 256
ROWS = 65536
N_STN = 16


def level_of(stream_key, shape, cuts, smallest, largest):
    def one(axis_at, blocks):
        steps = jax.random.uniform(jax.random.fold_in(jax.random.fold_in(stream_key, 6), axis_at), (blocks,), jnp.float32, smallest / len(cuts), largest / len(cuts))
        return jnp.repeat(jnp.exp(steps), shape[axis_at] // blocks).reshape((-1,) + (1,) * (len(shape) - axis_at - 1))

    loudness = one(*cuts[0])
    for cut in cuts[1:]:
        loudness = loudness * one(*cut)
    return loudness


def routed_block(key, own, number, rows, count, top, limit, lean):
    ranking = jax.random.permutation(key, count)
    packed, usual = shares(count, rows * top, limit, lean, True), shares(count, rows * top, limit, lean, False)
    places = jnp.arange(count)

    def named(lengths, offset_by):
        used = int((lengths > 0).sum())
        fixed = max(1, used // 4)
        moved = fixed + (places - fixed + offset_by * (used - fixed)) % max(1, count - fixed)
        return jnp.zeros((count,), jnp.int32).at[ranking[jnp.where(places < fixed, places, moved)]].set(jnp.asarray(lengths, jnp.int32))

    lengths = jnp.where(number % 4 == 0, named(packed, number // 4), named(usual, number - number // 4 - 1))
    mixed = jax.random.permutation(jax.random.fold_in(own, 3), count)
    giver, taker = mixed[0:count // 2 * 2:2], mixed[1:count // 2 * 2:2]
    slack = jnp.minimum(lengths[giver] - 1, limit - lengths[taker]) // 2
    slack = jnp.where((giver == ranking[0]) | (taker == ranking[0]) | (lengths[taker] == 0), 0, jnp.maximum(slack, 0))
    moved = jax.random.randint(jax.random.fold_in(own, 4), (count // 2,), 0, 1 << 20) % (slack + 1)
    lengths = lengths.at[giver].add(-moved).at[taker].add(moved)
    labels = jnp.searchsorted(jnp.cumsum(lengths), jnp.arange(rows * top), side="right").astype(jnp.int32)
    grid = labels.reshape(top, rows).T
    grid = grid[jax.random.permutation(jax.random.fold_in(own, 1), rows)]
    offset_by = jax.random.randint(jax.random.fold_in(own, 2), (rows, 1), 0, top)
    return jnp.take_along_axis(grid, (jnp.arange(top)[None, :] + offset_by) % top, axis=1)


def shares(amount, total, bound, lean, full):
    loads = [(1 << 20) // math.isqrt(rank ** lean) + 1 for rank in range(1, amount + 1)]
    largest = bound if full else min(bound, max(-(-total // amount), total * loads[0] // sum(loads)))
    least = 1 if total - largest >= amount - 1 else 0
    counts, rest = [largest] + [least] * (amount - 1), total - largest - least * (amount - 1)
    while rest > 0:
        movable = [i for i in range(1, amount) if counts[i] < largest] or [i for i in range(1, amount) if counts[i] < bound]
        mass, remaining = sum([loads[i] for i in movable]), rest
        for i in movable:
            addition = min(bound - counts[i], max(1, remaining * loads[i] // mass), rest)
            counts[i] = counts[i] + addition
            rest = rest - addition
    return np.array(counts)


def scatter_about(own_key, dims, scale, limit, pieces=(), held_as=jnp.bfloat16):
    loudness = level_of(own_key, dims, pieces, -0.22, 0.18) if pieces else 1.0
    entries = jax.random.normal(own_key, dims, jnp.float32) * scale * loudness
    return jnp.minimum(jnp.maximum(entries, -limit), limit).astype(held_as)


def setup_inputs(seed: int = 0, part: int = 0) -> dict:
    key_list = jax.random.split(jax.random.key(seed), 7)
    part_keys = jax.random.split(jax.random.fold_in(key_list[6], part), 7)
    station_partials = scatter_about(part_keys[0], (ROWS, P_SIZE), 1.0, 6.0, ((0, 16),))
    arc_partials = scatter_about(part_keys[1], (ROWS, P_SIZE), 1.0, 6.0, ((0, 16),))
    misclosure = scatter_about(part_keys[2], (ROWS,), 1.0, 6.0, ((0, 16),))
    arc_id_keys = jax.random.split(jax.random.fold_in(part_keys[3], 1), ROWS // OBS_DEV)
    arc_id_turns = jax.random.permutation(jax.random.fold_in(part_keys[3], 3), ROWS // OBS_DEV)
    arc_id = jax.vmap(lambda own, number: routed_block(jax.random.fold_in(part_keys[3], 2), own, number, OBS_DEV, ARCS, 1, CAP, 2))(arc_id_keys, arc_id_turns).reshape((ROWS, 1))
    arc_slot = jax.random.permutation(part_keys[4], ARCS).astype(jnp.int32)
    arc_prior = jnp.clip(jnp.exp(jax.random.uniform(part_keys[5], (ARCS,), jnp.float32, math.log(0.1), math.log(1.0))), 0.1, 1.0)
    return dict(station_partials=station_partials, arc_partials=arc_partials, misclosure=misclosure, arc_id=arc_id, arc_slot=arc_slot, arc_prior=arc_prior)


def bucket_rows(arc_ids, arc_slot, stn_rows, arc_rows, miss_rows):
    arc_table = jnp.arange(ARCS, dtype=jnp.int32)
    arc_match = (arc_ids[:, None] == arc_table[None, :]).astype(jnp.int32)
    slot_of_row = jnp.sum(arc_match * arc_slot[None, :], axis=1).astype(jnp.int32)
    onslot = (slot_of_row[:, None] == arc_table[None, :]).astype(jnp.int32)
    rank_in_slot = jnp.sum((jnp.cumsum(onslot, axis=0) - 1) * onslot, axis=1).astype(jnp.int32)
    positions = slot_of_row * CAP + rank_in_slot
    stn_buffer = jnp.zeros((ARCS * CAP, P_SIZE), stn_rows.dtype).at[positions].set(stn_rows)
    arc_buffer = jnp.zeros((ARCS * CAP, P_SIZE), arc_rows.dtype).at[positions].set(arc_rows)
    miss_buffer = jnp.zeros((ARCS * CAP,), miss_rows.dtype).at[positions].set(miss_rows)
    return (stn_buffer.reshape(ARCS, CAP, P_SIZE), arc_buffer.reshape(ARCS, CAP, P_SIZE), miss_buffer.reshape(ARCS, CAP))

def reference(station_partials, arc_partials, misclosure, arc_id, arc_slot, arc_prior):
    stn_all = station_partials.reshape(N_STN, OBS_DEV, P_SIZE)
    arc_all = arc_partials.reshape(N_STN, OBS_DEV, P_SIZE)
    miss_all = misclosure.reshape(N_STN, OBS_DEV)
    ids_all = arc_id.reshape(N_STN, OBS_DEV)
    prior_slot = jnp.zeros((ARCS,), jnp.float32).at[arc_slot].set(arc_prior)

    def gather_stats(carry, inputs):
        stn_rows, arc_rows, miss_rows, arc_ids = inputs
        stn_buffer, arc_buffer, miss_buffer = bucket_rows(arc_ids, arc_slot, stn_rows, arc_rows, miss_rows)
        arc_f = arc_buffer.astype(jnp.float32)
        normal_add = jnp.einsum('kcj,kcl->kjl', arc_f, arc_f)
        right_add = jnp.einsum('kcj,kc->kj', arc_f, miss_buffer.astype(jnp.float32))
        return ((carry[0] + normal_add, carry[1] + right_add), None)
    start_carry = (jnp.zeros((ARCS, P_SIZE, P_SIZE), jnp.float32), jnp.zeros((ARCS, P_SIZE), jnp.float32))
    (arc_normal, arc_right), _ = lax.scan(gather_stats, start_carry, (stn_all, arc_all, miss_all, ids_all))
    identity = jnp.eye(P_SIZE, dtype=jnp.float32)
    factor = jnp.linalg.cholesky(arc_normal + (prior_slot * OBS_DEV)[:, None, None] * identity)
    arc_whitened = jax.scipy.linalg.solve_triangular(factor, arc_right[..., None], lower=True)[..., 0]

    def per_station(inputs):
        stn_rows, arc_rows, miss_rows, arc_ids = inputs
        stn_buffer, arc_buffer, miss_buffer = bucket_rows(arc_ids, arc_slot, stn_rows, arc_rows, miss_rows)
        cross = jnp.einsum('kcj,kci->kji', arc_buffer.astype(jnp.float32), stn_buffer.astype(jnp.float32))
        white_cross = jax.scipy.linalg.solve_triangular(factor, cross, lower=True)
        schur_tile = jnp.einsum('kji,kjl->il', white_cross, white_cross, precision=lax.Precision.HIGHEST) / P_SIZE
        rhs_tile = jnp.einsum('kji,kj->i', white_cross, arc_whitened, precision=lax.Precision.HIGHEST) / P_SIZE
        own_normal = jnp.dot(stn_rows.T.astype(jnp.float32), stn_rows.astype(jnp.float32), preferred_element_type=jnp.float32) / OBS_DEV
        return (own_normal, schur_tile, rhs_tile)
    station_normal, elimination, elimination_rhs = lax.map(per_station, (stn_all, arc_all, miss_all, ids_all))
    return (station_normal, elimination, elimination_rhs, arc_whitened)
```

```python
import functools

import jax
import jax.numpy as jnp
from jax import lax
from jax.experimental import pallas as pl
from jax.experimental.pallas import tpu as pltpu
from jax.sharding import PartitionSpec as P

EXTRA = 8
NT = (((1,), (1,)), ((), ()))


def place_to_owner(place, bits):
    owner = 0
    for bit in range(bits):
        owner = owner | (((place >> bit) & 1) << (bits - 1 - bit))
    return owner


def arcs_of_slots(slot_ref, arc_ref, arcs):
    def put(arc, _):
        arc_ref[slot_ref[arc]] = arc
        return 0

    lax.fori_loop(0, arcs, put, 0)


def masked_pair(ids, first, second, table):
    def masked(arc):
        hit = jnp.where(ids == arc.astype(ids.dtype), 1, 0).astype(jnp.bfloat16)
        return (table * hit[None]).reshape(-1, table.shape[-1])

    return jnp.concatenate([masked(first), masked(second)], axis=0)


def spread_ids(id_ref, ids_sc):
    ids_sc[...] = jnp.broadcast_to(id_ref[...].astype(jnp.float32), ids_sc.shape)


def normals_kernel(bits, slot_ref, id_ref, miss_ref, arc_rows_ref, out_ref, arc_ref, ids_sc, left_sc):
    rows, width = arc_rows_ref.shape
    arcs = slot_ref.shape[0]
    me = lax.axis_index("stn")
    arcs_of_slots(slot_ref, arc_ref, arcs)
    spread_ids(id_ref, ids_sc)
    left_sc[0:width, :] = arc_rows_ref[...].T
    left_sc[width:, :] = jnp.broadcast_to(miss_ref[...], (16, rows))
    r = lax.broadcasted_iota(jnp.int32, (width, width), 0)
    c = lax.broadcasted_iota(jnp.int32, (width, width), 1)
    sub = lax.broadcasted_iota(jnp.int32, (EXTRA, width), 0)

    def one(place, _):
        owner = jnp.bitwise_xor(place_to_owner(place, bits), me)
        table = left_sc[0:width, :].reshape(width // 16, 16, rows)
        pair = masked_pair(ids_sc[...], arc_ref[2 * owner], arc_ref[2 * owner + 1], table)
        full = lax.dot_general(left_sc[...], pair, NT, preferred_element_type=jnp.float32)
        first, second = full[:width, :width], full[:width, width:]
        out_ref[place, 0:width, :] = jnp.where(r >= c, first, second)
        diag = jnp.sum(jnp.where(r == c, second, 0.0), axis=0, keepdims=True)
        tail = jnp.where(sub == 0, diag, 0.0)
        tail = jnp.where(sub == 1, full[width : width + 1, :width], tail)
        out_ref[place, width:, :] = jnp.where(sub == 2, full[width : width + 1, width:], tail)
        return 0

    lax.fori_loop(0, arcs // 2, one, 0)


def cross_kernel(bits, slot_ref, id_ref, stn_rows_ref, arc_rows_ref, out_ref, own_ref, arc_ref, ids_sc, table_sc, left_sc):
    rows, width = arc_rows_ref.shape
    arcs = slot_ref.shape[0]
    me = lax.axis_index("stn")
    arcs_of_slots(slot_ref, arc_ref, arcs)
    spread_ids(id_ref, ids_sc)
    table_sc[...] = arc_rows_ref[...].T
    left_sc[...] = stn_rows_ref[...].T
    own_ref[0] = lax.dot_general(
        left_sc[...], stn_rows_ref[...], (((1,), (0,)), ((), ())), preferred_element_type=jnp.float32
    ) / rows

    def one(place, _):
        owner = jnp.bitwise_xor(place_to_owner(place, bits), me)
        table = table_sc[...].reshape(width // 16, 16, rows)
        pair = masked_pair(ids_sc[...], arc_ref[2 * owner], arc_ref[2 * owner + 1], table)
        full = lax.dot_general(left_sc[...], pair, NT, preferred_element_type=jnp.float32)
        high = full.astype(jnp.bfloat16)
        low = (full - high.astype(jnp.float32)).astype(jnp.bfloat16)
        for half in range(2):
            cut = slice(half * width, (half + 1) * width)
            out_ref[2 * place + half, :, 0:width] = high[:, cut]
            out_ref[2 * place + half, :, width:] = low[:, cut]
        return 0

    lax.fori_loop(0, arcs // 2, one, 0)


def lanes_of(block, k):
    return jnp.broadcast_to(block[:, k : k + 1], block.shape)


def factor_kernel(rows, slot_ref, prior_ref, kept_ref, came_ref, out_ref, sys_sc):
    width = kept_ref.shape[-1]
    arcs = slot_ref.shape[0]
    me = lax.axis_index("stn")

    def find(arc, found):
        hit = slot_ref[arc]
        weight = prior_ref[arc]
        return (
            jnp.where(hit == 2 * me, weight, found[0]),
            jnp.where(hit == 2 * me + 1, weight, found[1]),
        )

    priors = lax.fori_loop(0, arcs, find, (jnp.float32(0), jnp.float32(0)))
    packed = kept_ref[0, 0:width, :] + came_ref[0, 0:width, :]
    tail = kept_ref[0, width:, :] + came_ref[0, width:, :]
    flipped = packed.T
    r = lax.broadcasted_iota(jnp.int32, (width, width), 0)
    c = lax.broadcasted_iota(jnp.int32, (width, width), 1)
    eye = r == c
    first = jnp.where(r >= c, packed, flipped)
    second = jnp.where(r < c, packed, flipped)
    second = jnp.where(eye, tail[0:1, :], second)
    sys_sc[0] = first + jnp.where(eye, priors[0] * rows, 0.0)
    sys_sc[1] = second + jnp.where(eye, priors[1] * rows, 0.0)
    tiles = width // 8
    sub = lax.broadcasted_iota(jnp.int32, (8, width), 0)
    lane = lax.broadcasted_iota(jnp.int32, (8, width), 1)
    state = [[sys_sc[m, 8 * t : 8 * t + 8, :] for t in range(tiles)] for m in range(2)]
    for k in range(width):
        kt, ks = k // 8, k % 8
        for m in range(2):
            tile = state[m]
            row = jnp.broadcast_to(tile[kt][ks : ks + 1, :], (8, width))
            inverse = 1.0 / lanes_of(row, k)
            scaled = jnp.where(lane == k, inverse, row * inverse)
            if ks < 7:
                below = sub > ks
                col = jnp.where(below, lanes_of(tile[kt], k), 0.0)
                base = jnp.where(below & (lane == k), 0.0, tile[kt])
                tile[kt] = base - col * scaled
            for t in range(kt + 1, tiles):
                col = lanes_of(tile[t], k)
                tile[t] = jnp.where(lane == k, 0.0, tile[t]) - col * scaled
    for m in range(2):
        for t in range(tiles):
            sys_sc[m, 8 * t : 8 * t + 8, :] = state[m][t]
    inverses = []
    for m in range(2):
        done = sys_sc[m]
        pivot = jnp.sum(jnp.where(eye, done, 0.0), axis=1, keepdims=True)
        scale = 1.0 / jnp.sqrt(pivot)
        inverses.append(jnp.where(r > c, done * scale, jnp.where(eye, scale, 0.0)))
    whitened = [
        lax.dot_general(
            tail, inverses[m], NT, precision=lax.Precision.HIGHEST, preferred_element_type=jnp.float32
        )[m + 1 : m + 2]
        for m in range(2)
    ]
    out_ref[0, 0:width, :] = jnp.where(r >= c, inverses[0], inverses[1].T)
    diag = jnp.sum(jnp.where(eye, inverses[1], 0.0), axis=0, keepdims=True)
    last = jnp.where(sub == 0, diag, 0.0)
    last = jnp.where(sub == 1, whitened[0], last)
    out_ref[0, width:, :] = jnp.where(sub == 2, whitened[1], last)


def split(value):
    high = value.astype(jnp.bfloat16)
    return high, (value - high.astype(jnp.float32)).astype(jnp.bfloat16)


def eliminate_kernel(counts, *refs):
    parts, (cross_ref, elim_ref, rhs_ref, sum_sc) = refs[: len(counts)], refs[len(counts) :]
    width = cross_ref.shape[1]
    r = lax.broadcasted_iota(jnp.int32, (width, width), 0)
    c = lax.broadcasted_iota(jnp.int32, (width, width), 1)
    sum_sc[...] = jnp.zeros_like(sum_sc)
    start = 0
    for part_ref, count in zip(parts, counts):

        def one(at, _, part_ref=part_ref, start=start):
            place = start + at
            packed = part_ref[at, 0:width, :]
            tail = part_ref[at, width:, :]
            second = jnp.where(r < c, packed, jnp.where(r == c, tail[0:1, :], 0.0)).T
            first = jnp.where(r >= c, packed, 0.0)
            highs, lows = [], []
            for half, factor in enumerate((first, second)):
                high, low = split(factor)
                right = jnp.concatenate(
                    [
                        jnp.concatenate([high, high], axis=1),
                        jnp.concatenate([low, jnp.zeros_like(low)], axis=1),
                    ],
                    axis=0,
                )
                both = lax.dot_general(
                    cross_ref[2 * place + half], right, NT, preferred_element_type=jnp.float32
                )
                high, low = split(both[:, :width] + both[:, width:])
                highs.append(high)
                lows.append(low)
            white_high, white_low = jnp.concatenate(highs, axis=1), jnp.concatenate(lows, axis=1)
            right = jnp.concatenate([white_high, white_low], axis=0)
            w_high, w_low = split(jnp.concatenate([tail[1:2], tail[2:3]], axis=1))
            rows16 = lax.broadcasted_iota(jnp.int32, (16, 2 * width), 0)
            w_rows = jnp.where(
                rows16 == 0,
                w_high.astype(jnp.float32),
                jnp.where(rows16 == 1, w_low.astype(jnp.float32), 0.0),
            ).astype(jnp.bfloat16)
            left = jnp.concatenate([white_high, w_rows], axis=0)
            sum_sc[...] += lax.dot_general(left, right, NT, preferred_element_type=jnp.float32)
            return 0

        lax.fori_loop(0, count, one, 0)
        start += count
    total = sum_sc[...]
    mixed = total[:width, width:]
    elim_ref[0] = (total[:width, :width] + (mixed + mixed.T)) / width
    w_part = total[width : width + 8]
    rhs_ref[...] = (w_part[0:1, :width] + w_part[0:1, width:] + w_part[1:2, :width]) / width


def body(station_partials, arc_partials, misclosure, arc_id, arc_slot, arc_prior):
    groups = lax.axis_size("stn")
    bits = groups.bit_length() - 1
    arcs = arc_slot.shape[0]
    rows, width = station_partials.shape
    ids = arc_id.reshape(1, rows)
    miss = misclosure.reshape(1, rows)
    smem = pl.BlockSpec(memory_space=pltpu.SMEM)
    vmem = pl.BlockSpec(memory_space=pltpu.VMEM)
    f32, bf16 = jnp.float32, jnp.bfloat16
    tall = width + EXTRA

    def swap(value, bit):
        return lax.ppermute(value, "stn", [(at, at ^ (1 << bit)) for at in range(groups)])

    normals = pl.pallas_call(
        functools.partial(normals_kernel, bits),
        out_shape=jax.ShapeDtypeStruct((groups, tall, width), f32),
        in_specs=[smem, vmem, vmem, vmem],
        out_specs=vmem,
        scratch_shapes=[
            pltpu.SMEM((arcs,), jnp.int32),
            pltpu.VMEM((16, rows), f32),
            pltpu.VMEM((width + 16, rows), bf16),
        ],
        name="normals",
    )(arc_slot, ids, miss, arc_partials)
    flops = 2 * rows * arcs * width * width
    crosses, station_normal = pl.pallas_call(
        functools.partial(cross_kernel, bits),
        out_shape=[
            jax.ShapeDtypeStruct((arcs, width, 2 * width), bf16),
            jax.ShapeDtypeStruct((1, width, width), f32),
        ],
        in_specs=[smem, vmem, vmem, vmem],
        out_specs=[vmem, vmem],
        scratch_shapes=[
            pltpu.SMEM((arcs,), jnp.int32),
            pltpu.VMEM((16, rows), f32),
            pltpu.VMEM((width, rows), bf16),
            pltpu.VMEM((width, rows), bf16),
        ],
        cost_estimate=pl.CostEstimate(flops=flops, bytes_accessed=8 * rows * width, transcendentals=0),
        name="cross",
    )(arc_slot, ids, station_partials, arc_partials)

    held = normals
    for bit in range(bits):
        half = held.shape[0] // 2
        came = swap(held[half:], bit)
        if bit < bits - 1:
            held = held[:half] + came
        else:
            held = held[:half]
    mine = pl.pallas_call(
        functools.partial(factor_kernel, float(rows)),
        out_shape=jax.ShapeDtypeStruct((1, tall, width), f32),
        in_specs=[smem, smem, vmem, vmem],
        out_specs=vmem,
        scratch_shapes=[pltpu.VMEM((2, width, width), f32)],
        name="factor",
    )(arc_slot, arc_prior, held, came)
    arc_whitened = mine[0, width + 1 : width + 3, :]
    pieces = [mine]
    for bit in reversed(range(bits)):
        pieces = pieces + [swap(piece, bit) for piece in pieces]
    elimination, elimination_rhs = pl.pallas_call(
        functools.partial(eliminate_kernel, tuple(piece.shape[0] for piece in pieces)),
        out_shape=[
            jax.ShapeDtypeStruct((1, width, width), f32),
            jax.ShapeDtypeStruct((1, width), f32),
        ],
        in_specs=[vmem] * (len(pieces) + 1),
        out_specs=[vmem, vmem],
        scratch_shapes=[pltpu.VMEM((width + 16, 2 * width), f32)],
        name="eliminate",
    )(*pieces, crosses)
    return (station_normal, elimination, elimination_rhs, arc_whitened)


def solution(mesh):
    in_specs = (
        P(("day", "stn"), None),
        P(("day", "stn"), None),
        P(("day", "stn")),
        P(("day", "stn"), None),
        P("day"),
        P("day"),
    )
    out_specs = (
        P(("day", "stn"), None, None),
        P(("day", "stn"), None, None),
        P(("day", "stn"), None),
        P(("day", "stn"), None),
    )
    return jax.shard_map(body, mesh=mesh, in_specs=in_specs, out_specs=out_specs, check_vma=False)
```

```python
import functools

import jax
import jax.numpy as jnp
from jax import lax
from jax.experimental import pallas as pl
from jax.experimental.pallas import tpu as pltpu
from jax.sharding import PartitionSpec as P


EXTRA = 8
LIMITED = pltpu.CompilerParams(vmem_limit_bytes=24 * 2**20)
NT = (((1,), (1,)), ((), ()))
NN = (((1,), (0,)), ((), ()))


def split(value):
    high = value.astype(jnp.bfloat16)
    return high, (value - high.astype(jnp.float32)).astype(jnp.bfloat16)


def arcs_of_slots(slot_ref, arc_ref, arcs):
    def put(arc, _):
        arc_ref[slot_ref[arc]] = arc
        return 0

    lax.fori_loop(0, arcs, put, 0)


def tiles_kernel(owners, want_table, want_own, *refs):
    slot_ref, id_ref, miss_ref, stn_rows_ref, arc_rows_ref = refs[:5]
    table_ref, sent_ref, kept_ref, cross_ref = refs[5:9]
    own_ref = refs[9] if want_own else None
    arc_ref, ids_sc = refs[-2:]
    rows, width = arc_rows_ref.shape
    arcs = slot_ref.shape[0]
    me = lax.axis_index("stn")
    arcs_of_slots(slot_ref, arc_ref, arcs)
    ids_sc[...] = jnp.broadcast_to(id_ref[...].astype(jnp.float32), ids_sc.shape)
    if want_table:
        table_ref[...] = arc_rows_ref[...].T
    mine = []
    for owner in owners:
        first = 2 * jnp.bitwise_xor(me, owner)
        mine += [arc_ref[first], arc_ref[first + 1]]
    sub16 = lax.broadcasted_iota(jnp.int32, ids_sc.shape, 0)
    named = jnp.full(ids_sc.shape, -1.0, jnp.float32)
    left = []
    for at, arc in enumerate(mine):
        arc = arc.astype(jnp.float32)
        hit = jnp.where(ids_sc[...] == arc, 1.0, 0.0).astype(jnp.bfloat16)
        table = table_ref[...].reshape(width // 16, 16, rows)
        left.append((table * hit[None]).reshape(width, rows))
        named = jnp.where(sub16 == at, arc, named)
    hit = jnp.where(ids_sc[...] == named, 1.0, 0.0).astype(jnp.bfloat16)
    miss = miss_ref[...].astype(jnp.float32)
    miss = jnp.concatenate([miss[at : at + 1] for at in range(miss.shape[0])], axis=1)
    left.append(hit * jnp.broadcast_to(miss, hit.shape).astype(jnp.bfloat16))
    right = jnp.concatenate([arc_rows_ref[...], stn_rows_ref[...]], axis=1)
    full = lax.dot_general(
        jnp.concatenate(left, axis=0), right, NN, preferred_element_type=jnp.float32
    )
    r = lax.broadcasted_iota(jnp.int32, (width, width), 0)
    c = lax.broadcasted_iota(jnp.int32, (width, width), 1)
    sub = lax.broadcasted_iota(jnp.int32, (EXTRA, width), 0)
    rights = full[len(mine) * width :, :width]
    half = len(owners) // 2
    for at in range(len(owners)):
        top = 2 * at * width
        first, second = full[top : top + width, :width], full[top + width : top + 2 * width, :width]
        out_ref = sent_ref if at < half else kept_ref
        out_ref[at % half, 0:width, :] = jnp.where(r >= c, first, second)
        diag = jnp.sum(jnp.where(r == c, second, 0.0), axis=0, keepdims=True)
        tail = jnp.where(sub == 0, diag, 0.0)
        tail = jnp.where(sub == 1, rights[2 * at : 2 * at + 1], tail)
        out_ref[at % half, width:, :] = jnp.where(sub == 2, rights[2 * at + 1 : 2 * at + 2], tail)
        for side in range(2):
            cross = full[top + side * width : top + (side + 1) * width, width:]
            cross_ref[2 * at + side, :, :width], cross_ref[2 * at + side, :, width:] = split(cross)
    if want_own:
        own = lax.dot_general(
            stn_rows_ref[...].T, stn_rows_ref[...], NN, preferred_element_type=jnp.float32
        )
        own_ref[0] = own / rows


def lanes_of(block, k):
    return jnp.broadcast_to(block[:, k : k + 1], block.shape)


def rows_of(block, k):
    return jnp.broadcast_to(block[k : k + 1, :], block.shape)


def inverse_root(value):
    guess = lax.rsqrt(value)
    return guess * (1.5 - 0.5 * value * guess * guess)


def eliminate_panel(tile, panel, sub, lane):
    base = 8 * panel
    inside = (lane >= base) & (lane < base + 8)
    top = tile[panel]
    columns = [lanes_of(top, base + j) for j in range(8)]
    low = {(i, j): rows_of(columns[j], i) for j in range(8) for i in range(j, 8)}
    start = jnp.where(inside, jnp.where(lane - base == sub, 1.0, 0.0), top)
    white = [rows_of(start, i) for i in range(8)]
    root = []
    for j in range(8):
        root.append(inverse_root(low[j, j]))
        for i in range(j + 1, 8):
            low[i, j] = low[i, j] * root[j]
        for k in range(j + 1, 8):
            for i in range(k, 8):
                low[i, k] = low[i, k] - low[i, j] * low[k, j]
        white[j] = white[j] * root[j]
        for i in range(j + 1, 8):
            white[i] = white[i] - low[i, j] * white[j]
    done = white[0]
    for j in range(1, 8):
        done = jnp.where(sub == j, white[j], done)
    tile[panel] = done
    if panel + 1 == len(tile):
        return
    back = list(white)
    for j in reversed(range(8)):
        back[j] = back[j] * root[j]
        for i in range(j):
            back[i] = back[i] - low[j, i] * back[j]
    for t in range(panel + 1, len(tile)):
        rest = jnp.where(inside, 0.0, tile[t])
        for j in reversed(range(8)):
            rest = rest - lanes_of(tile[t], base + j) * back[j]
        tile[t] = rest


def factor_kernel(rows, slot_ref, prior_ref, *refs):
    (out_ref, sys_sc), terms = refs[-2:], refs[:-2]
    width = out_ref.shape[-1]
    arcs = slot_ref.shape[0]
    me = lax.axis_index("stn")

    def find(arc, found):
        hit = slot_ref[arc]
        weight = prior_ref[arc]
        return (
            jnp.where(hit == 2 * me, weight, found[0]),
            jnp.where(hit == 2 * me + 1, weight, found[1]),
        )

    priors = lax.fori_loop(0, arcs, find, (jnp.float32(0), jnp.float32(0)))
    whole = sum([term[0] for term in terms[1:]], terms[0][0])
    packed, tail = whole[:width], whole[width:]
    flipped = packed.T
    r = lax.broadcasted_iota(jnp.int32, (width, width), 0)
    c = lax.broadcasted_iota(jnp.int32, (width, width), 1)
    eye = r == c
    first = jnp.where(r >= c, packed, flipped)
    second = jnp.where(r < c, packed, flipped)
    second = jnp.where(eye, tail[0:1, :], second)
    sys_sc[0] = first + jnp.where(eye, priors[0] * rows, 0.0)
    sys_sc[1] = second + jnp.where(eye, priors[1] * rows, 0.0)
    tiles = width // 8
    sub = lax.broadcasted_iota(jnp.int32, (8, width), 0)
    lane = lax.broadcasted_iota(jnp.int32, (8, width), 1)
    state = [[sys_sc[m, 8 * t : 8 * t + 8, :] for t in range(tiles)] for m in range(2)]
    for panel in range(tiles):
        for m in range(2):
            eliminate_panel(state[m], panel, sub, lane)
    for m in range(2):
        for t in range(tiles):
            sys_sc[m, 8 * t : 8 * t + 8, :] = state[m][t]
    inverses = [jnp.where(r >= c, sys_sc[m], 0.0) for m in range(2)]
    whitened = [
        lax.dot_general(
            tail, inverses[m], NT, precision=lax.Precision.HIGHEST, preferred_element_type=jnp.float32
        )[m + 1 : m + 2]
        for m in range(2)
    ]
    out_ref[0, 0:width, :] = jnp.where(r >= c, inverses[0], inverses[1].T)
    diag = jnp.sum(jnp.where(eye, inverses[1], 0.0), axis=0, keepdims=True)
    last = jnp.where(sub == 0, diag, 0.0)
    last = jnp.where(sub == 1, whitened[0], last)
    out_ref[0, width:, :] = jnp.where(sub == 2, whitened[1], last)


def eliminate_kernel(places, *refs):
    pieces, refs = refs[: len(places)], refs[len(places) :]
    crosses, (elim_ref, rhs_ref, sum_sc) = refs[:-3], refs[-3:]
    width = elim_ref.shape[1]
    r = lax.broadcasted_iota(jnp.int32, (width, width), 0)
    c = lax.broadcasted_iota(jnp.int32, (width, width), 1)
    rows16 = lax.broadcasted_iota(jnp.int32, (16, 2 * width), 0)
    for count, (piece_ref, (chunk, at)) in enumerate(zip(pieces, places)):
        packed = piece_ref[0, 0:width, :]
        tail = piece_ref[0, width:, :]
        second = jnp.where(r < c, packed, jnp.where(r == c, tail[0:1, :], 0.0)).T
        first = jnp.where(r >= c, packed, 0.0)
        highs, lows = [], []
        for side, factor in enumerate((first, second)):
            left = jnp.concatenate(split(factor), axis=1)
            cross = crosses[chunk][2 * at + side]
            kept = jnp.concatenate([cross[:, :width], jnp.zeros((width, width), cross.dtype)], axis=1)
            both = lax.dot_general(
                left, jnp.concatenate([cross, kept], axis=0), NN, preferred_element_type=jnp.float32
            )
            high, low = split(both[:, :width] + both[:, width:])
            highs.append(high)
            lows.append(low)
        white_high, white_low = jnp.concatenate(highs, axis=0), jnp.concatenate(lows, axis=0)
        right = jnp.concatenate([white_high, white_low], axis=1)
        w_high, w_low = split(jnp.concatenate([tail[1:2], tail[2:3]], axis=1))
        w_rows = jnp.where(
            rows16 == 0,
            w_high.astype(jnp.float32),
            jnp.where(rows16 == 1, w_low.astype(jnp.float32), 0.0),
        ).astype(jnp.bfloat16)
        left = jnp.concatenate([white_high.T, w_rows], axis=0)
        term = lax.dot_general(left, right, NN, preferred_element_type=jnp.float32)
        if count:
            sum_sc[...] += term
        else:
            sum_sc[...] = term
    total = sum_sc[...]
    mixed = total[:width, width:]
    elim_ref[0] = (total[:width, :width] + (mixed + mixed.T)) / width
    w_part = total[width : width + 8]
    rhs_ref[...] = (w_part[0:1, :width] + w_part[0:1, width:] + w_part[1:2, :width]) / width


def body(station_partials, arc_partials, misclosure, arc_id, arc_slot, arc_prior):
    groups = lax.axis_size("stn")
    bits = groups.bit_length() - 1
    arcs = arc_slot.shape[0]
    rows, width = station_partials.shape
    ids = arc_id.reshape(1, rows)
    miss = misclosure.reshape(rows // width, width)
    smem = pl.BlockSpec(memory_space=pltpu.SMEM)
    vmem = pl.BlockSpec(memory_space=pltpu.VMEM)
    f32, bf16 = jnp.float32, jnp.bfloat16
    tall = width + EXTRA

    def swap(value, flip):
        return lax.ppermute(value, "stn", [(at, at ^ flip) for at in range(groups)])

    chunks = groups // 4
    crosses, where, terms = [], {}, []
    for chunk in range(chunks):
        far = groups - 4 * (chunk + 1)
        owners = [far + 1, far + 3, far, far + 2]
        want_own = chunk == chunks - 1
        shapes = [
            jax.ShapeDtypeStruct((2, tall, width), f32),
            jax.ShapeDtypeStruct((2, tall, width), f32),
            jax.ShapeDtypeStruct((2 * len(owners), width, 2 * width), bf16),
        ]
        if chunk == 0:
            shapes.insert(0, jax.ShapeDtypeStruct((width, rows), bf16))
        if want_own:
            shapes.append(jax.ShapeDtypeStruct((1, width, width), f32))
        operands = [arc_slot, ids, miss, station_partials, arc_partials]
        if chunk:
            operands.append(table)
        found = pl.pallas_call(
            functools.partial(tiles_kernel, tuple(owners), chunk == 0, want_own),
            out_shape=shapes,
            in_specs=[smem] + [vmem] * (len(operands) - 1),
            out_specs=[vmem] * len(shapes),
            scratch_shapes=[pltpu.SMEM((arcs,), jnp.int32), pltpu.VMEM((16, rows), f32)],
            cost_estimate=pl.CostEstimate(
                flops=2 * rows * 2 * len(owners) * width * 2 * width,
                bytes_accessed=4 * rows * width,
                transcendentals=0,
            ),
            compiler_params=LIMITED,
            name="tiles",
        )(*operands)
        if chunk == 0:
            table, found = found[0], found[1:]
        sent, kept, cross, *own = found
        crosses.append(cross)
        where.update({owner: (chunk, at) for at, owner in enumerate(owners)})
        came = swap(sent, 1)
        for at, owner in enumerate(owners[2:]):
            if owner:
                both = kept[at : at + 1] + came[at : at + 1]
                terms.append(swap(both, owner))
            else:
                terms += [kept[at : at + 1], came[at : at + 1]]
    (station_normal,) = own
    mine = pl.pallas_call(
        functools.partial(factor_kernel, float(rows)),
        out_shape=jax.ShapeDtypeStruct((1, tall, width), f32),
        in_specs=[smem, smem] + [vmem] * len(terms),
        out_specs=vmem,
        scratch_shapes=[pltpu.VMEM((2, width, width), f32)],
        compiler_params=LIMITED,
        name="factor",
    )(arc_slot, arc_prior, *terms)
    arc_whitened = mine[0, width + 1 : width + 3, :]
    pieces = {0: mine}
    for bit in reversed(range(bits)):
        pieces.update({owner ^ (1 << bit): swap(piece, 1 << bit) for owner, piece in pieces.items()})
    elimination, elimination_rhs = pl.pallas_call(
        functools.partial(eliminate_kernel, tuple(where[owner] for owner in pieces)),
        out_shape=[
            jax.ShapeDtypeStruct((1, width, width), f32),
            jax.ShapeDtypeStruct((1, width), f32),
        ],
        in_specs=[vmem] * (len(pieces) + chunks),
        out_specs=[vmem, vmem],
        scratch_shapes=[pltpu.VMEM((width + 16, 2 * width), f32)],
        compiler_params=LIMITED,
        name="eliminate",
    )(*pieces.values(), *crosses)
    return (station_normal, elimination, elimination_rhs, arc_whitened)


def solution(mesh):
    in_specs = (
        P(("day", "stn"), None),
        P(("day", "stn"), None),
        P(("day", "stn")),
        P(("day", "stn"), None),
        P("day"),
        P("day"),
    )
    out_specs = (
        P(("day", "stn"), None, None),
        P(("day", "stn"), None, None),
        P(("day", "stn"), None),
        P(("day", "stn"), None),
    )
    return jax.shard_map(body, mesh=mesh, in_specs=in_specs, out_specs=out_specs, check_vma=False)
```

```python
import functools

import jax
import jax.numpy as jnp
from jax import lax
from jax.experimental import pallas as pl
from jax.experimental.pallas import tpu as pltpu
from jax.sharding import PartitionSpec as P


EXTRA = 8
LIMITED = pltpu.CompilerParams(vmem_limit_bytes=24 * 2**20)
NT = (((1,), (1,)), ((), ()))
NN = (((1,), (0,)), ((), ()))


def split(value):
    high = value.astype(jnp.bfloat16)
    return high, (value - high.astype(jnp.float32)).astype(jnp.bfloat16)


def arcs_of_slots(slot_ref, arc_ref, arcs):
    def put(arc, _):
        arc_ref[slot_ref[arc]] = arc
        return 0

    lax.fori_loop(0, arcs, put, 0)


def tiles_kernel(owners, first, last, *refs):
    if first:
        slot_any, id_any, miss_any, stn_any, arc_any = refs[:5]
        table_ref, rows_ref, sent_ref, kept_ref, cross_ref = refs[5:10]
        arc_ref, ids_sc, slot_ref, id_ref, miss_ref, sems = refs[10:]
        width = arc_any.shape[1]
        moves = [
            pltpu.make_async_copy(source, target, sems.at[at])
            for at, (source, target) in enumerate(
                [
                    (slot_any, slot_ref),
                    (arc_any, rows_ref.at[:, pl.ds(0, width)]),
                    (id_any, id_ref),
                    (miss_any, miss_ref),
                    (stn_any, rows_ref.at[:, pl.ds(width, width)]),
                ]
            )
        ]
        for move in moves:
            move.start()
    else:
        slot_ref, id_ref, miss_ref, table_ref, rows_ref = refs[:5]
        prior_ref = refs[5] if last else None
        sent_ref, kept_ref, cross_ref, arc_ref, ids_sc = refs[-5:]
    rows, width = rows_ref.shape[0], rows_ref.shape[1] // 2
    arcs = slot_ref.shape[0]
    me = lax.axis_index("stn")
    if first:
        moves[0].wait()
    arcs_of_slots(slot_ref, arc_ref, arcs)
    if first:
        moves[1].wait()
        table_ref[...] = rows_ref[:, 0:width].T
        for move in moves[2:]:
            move.wait()
    ids_sc[...] = jnp.broadcast_to(id_ref[...].astype(jnp.float32), ids_sc.shape)
    mine = []
    for owner in owners:
        slot = 2 * jnp.bitwise_xor(me, owner)
        mine += [arc_ref[slot], arc_ref[slot + 1]]
    sub16 = lax.broadcasted_iota(jnp.int32, ids_sc.shape, 0)
    named = jnp.full(ids_sc.shape, -1.0, jnp.float32)
    left = []
    for at, arc in enumerate(mine):
        arc = arc.astype(jnp.float32)
        hit = jnp.where(ids_sc[...] == arc, 1.0, 0.0).astype(jnp.bfloat16)
        table = table_ref[...].reshape(width // 16, 16, rows)
        left.append((table * hit[None]).reshape(width, rows))
        named = jnp.where(sub16 == at, arc, named)
    hit = jnp.where(ids_sc[...] == named, 1.0, 0.0).astype(jnp.bfloat16)
    miss = miss_ref[...].astype(jnp.float32)
    miss = jnp.concatenate([miss[at : at + 1] for at in range(miss.shape[0])], axis=1)
    left.append(hit * jnp.broadcast_to(miss, hit.shape).astype(jnp.bfloat16))
    full = lax.dot_general(
        jnp.concatenate(left, axis=0), rows_ref[...], NN, preferred_element_type=jnp.float32
    )
    r = lax.broadcasted_iota(jnp.int32, (width, width), 0)
    c = lax.broadcasted_iota(jnp.int32, (width, width), 1)
    sub = lax.broadcasted_iota(jnp.int32, (EXTRA, width), 0)
    rights = full[len(mine) * width :, :width]
    half = len(owners) // 2
    for at in range(len(owners)):
        top = 2 * at * width
        lower, upper = full[top : top + width, :width], full[top + width : top + 2 * width, :width]
        out_ref = sent_ref if at < half else kept_ref
        out_ref[at % half, 0:width, :] = jnp.where(r >= c, lower, upper)
        diag = jnp.sum(jnp.where(r == c, upper, 0.0), axis=0, keepdims=True)
        tail = jnp.where(sub == 0, diag, 0.0)
        tail = jnp.where(sub == 1, rights[2 * at : 2 * at + 1], tail)
        tail = jnp.where(sub == 2, rights[2 * at + 1 : 2 * at + 2], tail)
        if last and owners[at] == 0:
            for side in range(2):
                tail = jnp.where(sub == 3 + side, prior_ref[mine[2 * at + side]] * rows, tail)
        out_ref[at % half, width:, :] = tail
        for side in range(2):
            cross = full[top + side * width : top + (side + 1) * width, width:]
            cross_ref[2 * at + side, :, :width], cross_ref[2 * at + side, :, width:] = split(cross)


def own_kernel(rows_ref, out_ref):
    rows = rows_ref[...]
    own = lax.dot_general(rows.T, rows, NN, preferred_element_type=jnp.float32)
    out_ref[0] = own / rows.shape[0]


def lanes_of(block, k):
    return jnp.broadcast_to(block[:, k : k + 1], block.shape)


def rows_of(block, k):
    return jnp.broadcast_to(block[k : k + 1, :], block.shape)


def inverse_root(value):
    guess = lax.rsqrt(value)
    return guess * (1.5 - 0.5 * value * guess * guess)


def eliminate_panel(tile, panel, sub, lane):
    base = 8 * panel
    inside = (lane >= base) & (lane < base + 8)
    top = tile[panel]
    columns = [lanes_of(top, base + j) for j in range(8)]
    low = {(i, j): rows_of(columns[j], i) for j in range(8) for i in range(j, 8)}
    start = jnp.where(inside, jnp.where(lane - base == sub, 1.0, 0.0), top)
    white = [rows_of(start, i) for i in range(8)]
    root = []
    for j in range(8):
        root.append(inverse_root(low[j, j]))
        for i in range(j + 1, 8):
            low[i, j] = low[i, j] * root[j]
        for k in range(j + 1, 8):
            for i in range(k, 8):
                low[i, k] = low[i, k] - low[i, j] * low[k, j]
        white[j] = white[j] * root[j]
        for i in range(j + 1, 8):
            white[i] = white[i] - low[i, j] * white[j]
    done = white[0]
    for j in range(1, 8):
        done = jnp.where(sub == j, white[j], done)
    tile[panel] = done
    if panel + 1 == len(tile):
        return
    back = list(white)
    for j in reversed(range(8)):
        back[j] = back[j] * root[j]
        for i in range(j):
            back[i] = back[i] - low[j, i] * back[j]
    for t in range(panel + 1, len(tile)):
        rest = jnp.where(inside, 0.0, tile[t])
        for j in reversed(range(8)):
            rest = rest - lanes_of(tile[t], base + j) * back[j]
        tile[t] = rest


def factor_kernel(*refs):
    (out_ref, sys_sc), terms = refs[-2:], refs[:-2]
    width = out_ref.shape[-1]
    whole = sum([term[0] for term in terms[1:]], terms[0][0])
    packed, tail = whole[:width], whole[width:]
    flipped = packed.T
    r = lax.broadcasted_iota(jnp.int32, (width, width), 0)
    c = lax.broadcasted_iota(jnp.int32, (width, width), 1)
    eye = r == c
    first = jnp.where(r >= c, packed, flipped)
    second = jnp.where(r < c, packed, flipped)
    second = jnp.where(eye, tail[0:1, :], second)
    sys_sc[0] = first + jnp.where(eye, tail[3:4, :], 0.0)
    sys_sc[1] = second + jnp.where(eye, tail[4:5, :], 0.0)
    tiles = width // 8
    sub = lax.broadcasted_iota(jnp.int32, (8, width), 0)
    lane = lax.broadcasted_iota(jnp.int32, (8, width), 1)
    state = [[sys_sc[m, 8 * t : 8 * t + 8, :] for t in range(tiles)] for m in range(2)]
    for panel in range(tiles):
        for m in range(2):
            eliminate_panel(state[m], panel, sub, lane)
    for m in range(2):
        for t in range(tiles):
            sys_sc[m, 8 * t : 8 * t + 8, :] = state[m][t]
    inverses = [jnp.where(r >= c, sys_sc[m], 0.0) for m in range(2)]
    whitened = [
        lax.dot_general(
            tail, inverses[m], NT, precision=lax.Precision.HIGHEST, preferred_element_type=jnp.float32
        )[m + 1 : m + 2]
        for m in range(2)
    ]
    out_ref[0, 0:width, :] = jnp.where(r >= c, inverses[0], inverses[1].T)
    diag = jnp.sum(jnp.where(eye, inverses[1], 0.0), axis=0, keepdims=True)
    last = jnp.where(sub == 0, diag, 0.0)
    last = jnp.where(sub == 1, whitened[0], last)
    out_ref[0, width:, :] = jnp.where(sub == 2, whitened[1], last)


def eliminate_kernel(places, added, last, *refs):
    pieces, refs = refs[: len(places)], refs[len(places) :]
    before, refs = refs[:added], refs[added:]
    if last:
        crosses, (elim_ref, rhs_ref, sum_sc) = refs[:-3], refs[-3:]
    else:
        crosses, sum_sc = refs[:-1], refs[-1]
    width = sum_sc.shape[1] // 2
    r = lax.broadcasted_iota(jnp.int32, (width, width), 0)
    c = lax.broadcasted_iota(jnp.int32, (width, width), 1)
    rows16 = lax.broadcasted_iota(jnp.int32, (16, 2 * width), 0)
    for count, (piece_ref, (chunk, at)) in enumerate(zip(pieces, places)):
        packed = piece_ref[0, 0:width, :]
        tail = piece_ref[0, width:, :]
        second = jnp.where(r < c, packed, jnp.where(r == c, tail[0:1, :], 0.0)).T
        first = jnp.where(r >= c, packed, 0.0)
        highs, lows = [], []
        for side, factor in enumerate((first, second)):
            left = jnp.concatenate(split(factor), axis=1)
            cross = crosses[chunk][2 * at + side]
            kept = jnp.concatenate([cross[:, :width], jnp.zeros((width, width), cross.dtype)], axis=1)
            both = lax.dot_general(
                left, jnp.concatenate([cross, kept], axis=0), NN, preferred_element_type=jnp.float32
            )
            high, low = split(both[:, :width] + both[:, width:])
            highs.append(high)
            lows.append(low)
        white_high, white_low = jnp.concatenate(highs, axis=0), jnp.concatenate(lows, axis=0)
        right = jnp.concatenate([white_high, white_low], axis=1)
        w_high, w_low = split(jnp.concatenate([tail[1:2], tail[2:3]], axis=1))
        w_rows = jnp.where(
            rows16 == 0,
            w_high.astype(jnp.float32),
            jnp.where(rows16 == 1, w_low.astype(jnp.float32), 0.0),
        ).astype(jnp.bfloat16)
        left = jnp.concatenate([white_high.T, w_rows], axis=0)
        term = lax.dot_general(left, right, NN, preferred_element_type=jnp.float32)
        if count:
            sum_sc[...] += term
        else:
            sum_sc[...] = sum([ref[...] for ref in before], term)
    if not last:
        return
    total = sum_sc[...]
    mixed = total[:width, width:]
    elim_ref[0] = (total[:width, :width] + (mixed + mixed.T)) / width
    w_part = total[width : width + 8]
    rhs_ref[...] = (w_part[0:1, :width] + w_part[0:1, width:] + w_part[1:2, :width]) / width


def body(station_partials, arc_partials, misclosure, arc_id, arc_slot, arc_prior):
    groups = lax.axis_size("stn")
    bits = groups.bit_length() - 1
    arcs = arc_slot.shape[0]
    rows, width = station_partials.shape
    ids = arc_id.reshape(1, rows)
    miss = misclosure.reshape(rows // width, width)
    smem = pl.BlockSpec(memory_space=pltpu.SMEM)
    vmem = pl.BlockSpec(memory_space=pltpu.VMEM)
    f32, bf16 = jnp.float32, jnp.bfloat16
    tall = width + EXTRA

    def swap(value, flip):
        return lax.ppermute(value, "stn", [(at, at ^ flip) for at in range(groups)])

    chunks = groups // 4
    crosses, where, terms = [], {}, []
    for chunk in range(chunks):
        far = groups - 4 * (chunk + 1)
        owners = [far + 1, far + 3, far, far + 2]
        shapes = [
            jax.ShapeDtypeStruct((2, tall, width), f32),
            jax.ShapeDtypeStruct((2, tall, width), f32),
            jax.ShapeDtypeStruct((2 * len(owners), width, 2 * width), bf16),
        ]
        scratch = [pltpu.SMEM((arcs,), jnp.int32), pltpu.VMEM((16, rows), f32)]
        first, last = chunk == 0, chunk == chunks - 1
        if first:
            shapes = [
                jax.ShapeDtypeStruct((width, rows), bf16),
                jax.ShapeDtypeStruct((rows, 2 * width), bf16),
            ] + shapes
            scratch += [
                pltpu.SMEM((arcs,), jnp.int32),
                pltpu.VMEM(ids.shape, ids.dtype),
                pltpu.VMEM(miss.shape, miss.dtype),
                pltpu.SemaphoreType.DMA((5,)),
            ]
            held = [arc_slot, ids, miss, station_partials, arc_partials]
            held = [pltpu.with_memory_space_constraint(value, pltpu.HBM) for value in held]
            operands = held
            in_specs = [pl.BlockSpec(memory_space=pltpu.HBM)] * 5
        else:
            operands = [arc_slot, ids, miss, *shared]
            in_specs = [smem] + [vmem] * 4
            if last:
                operands.append(arc_prior)
                in_specs.append(smem)
        found = pl.pallas_call(
            functools.partial(tiles_kernel, tuple(owners), first, last),
            out_shape=shapes,
            in_specs=in_specs,
            out_specs=[vmem] * len(shapes),
            scratch_shapes=scratch,
            cost_estimate=pl.CostEstimate(
                flops=2 * rows * 2 * len(owners) * width * 2 * width,
                bytes_accessed=4 * rows * width,
                transcendentals=0,
            ),
            compiler_params=LIMITED,
            name="tiles",
        )(*operands)
        if first:
            shared, found = found[:2], found[2:]
        sent, kept, cross = found
        crosses.append(cross)
        where.update({owner: (chunk, at) for at, owner in enumerate(owners)})
        came = swap(sent, 1)
        for at, owner in enumerate(owners[2:]):
            if owner:
                both = kept[at : at + 1] + came[at : at + 1]
                terms.append(swap(both, owner))
            else:
                terms += [kept[at : at + 1], came[at : at + 1]]
    mine = pl.pallas_call(
        factor_kernel,
        out_shape=jax.ShapeDtypeStruct((1, tall, width), f32),
        in_specs=[vmem] * len(terms),
        out_specs=vmem,
        scratch_shapes=[pltpu.VMEM((2, width, width), f32)],
        compiler_params=LIMITED,
        name="factor",
    )(*terms)
    arc_whitened = mine[0, width + 1 : width + 3, :]
    pieces = {0: mine}
    for bit in reversed(range(bits)):
        came = {}
        for owner, piece in pieces.items():
            came[owner ^ (1 << bit)] = swap(piece, 1 << bit)
        pieces.update(came)
    station_normal = pl.pallas_call(
        own_kernel,
        out_shape=jax.ShapeDtypeStruct((1, width, width), f32),
        in_specs=[vmem],
        out_specs=vmem,
        compiler_params=LIMITED,
        name="own",
    )(station_partials)
    late = list(pieces)[-1]
    soon = [owner for owner in pieces if not owner & 2]
    then = [owner for owner in pieces if owner & 2 and owner != late]
    before = []
    for group in (soon, then):
        before = [
            pl.pallas_call(
                functools.partial(eliminate_kernel, tuple(where[owner] for owner in group), len(before), False),
                out_shape=jax.ShapeDtypeStruct((width + 16, 2 * width), f32),
                in_specs=[vmem] * (len(group) + len(before) + chunks),
                out_specs=vmem,
                compiler_params=LIMITED,
            )(*[pieces[owner] for owner in group], *before, *crosses)
        ]
    elimination, elimination_rhs = pl.pallas_call(
        functools.partial(eliminate_kernel, (where[late],), 1, True),
        out_shape=[
            jax.ShapeDtypeStruct((1, width, width), f32),
            jax.ShapeDtypeStruct((1, width), f32),
        ],
        in_specs=[vmem] * (2 + chunks),
        out_specs=[vmem, vmem],
        scratch_shapes=[pltpu.VMEM((width + 16, 2 * width), f32)],
        compiler_params=LIMITED,
        name="eliminate",
    )(pieces[late], *before, *crosses)
    return (station_normal, elimination, elimination_rhs, arc_whitened)


def solution(mesh):
    in_specs = (
        P(("day", "stn"), None),
        P(("day", "stn"), None),
        P(("day", "stn")),
        P(("day", "stn"), None),
        P("day"),
        P("day"),
    )
    out_specs = (
        P(("day", "stn"), None, None),
        P(("day", "stn"), None, None),
        P(("day", "stn"), None),
        P(("day", "stn"), None),
    )
    return jax.shard_map(body, mesh=mesh, in_specs=in_specs, out_specs=out_specs, check_vma=False)
```
